32 devices in a mesh: gz: 4 (over y, x), gx: 2 (over core), gy: 4 (over z).
Axes of the slice: x: 2, y: 2, z: 4, core: 2. Of those that a mesh axis runs over, the one named last changes fastest.
Arguments:
- e_field: float32 [3, 24, 128, 512], P(None, 'gx', 'gy', 'gz'), may hold values from -6 to 6
- h_field: float32 [3, 24, 128, 512], P(None, 'gx', 'gy', 'gz'), may hold values from -6 to 6
- material: int32 [24, 128, 512], P('gx', 'gy', 'gz'), may hold values 0 or 1
- coef_index: int32 [24, 128, 512], P('gx', 'gy', 'gz'), may hold values from 0 to 15
- table_h: float32 [16, 3], replicated, may hold values from 0.15 to 0.6
- table_e: float32 [16, 3], replicated, may hold values from 0.15 to 0.55
- pickup: float32 [512], P('gz'), may hold values from -0.25 to 0.25
Outputs:
- electric_out: float32 [3, 24, 128, 512], P(None, 'gx', 'gy', 'gz')
- magnetic_out: float32 [3, 24, 128, 512], P(None, 'gx', 'gy', 'gz')
- wake_map: float32 [24, 128], P('gx', 'gy')
The draws below stay inside these ranges and needn't reach their ends.
All inputs are finite; a program needn't handle non-finite values. No bound on the sum of `material` on one device may be relied on, other than what follows from the above.
Results may differ from the reference program's by a relative error of at most 0.0001.
Values sent between devices are 32-bit elements; how exact they have to be, the bound alone decides.
No kernel may reach another device: no remote copies, remote signals or barrier semaphores. Data moves between devices by JAX's collectives and lax.ppermute only.
A program may use at most 64 MiB of HBM per device.

```python
import math
import jax
import jax.numpy as jnp
from jax import lax

NTAB = 16
NX = 24
NY = 128
NZ = 512


def with_ends(drawn, rng, least, high):
    shape = drawn.shape
    spot = [jax.random.randint(jax.random.fold_in(rng, axis), (), 0, shape[axis]) for axis in range(len(shape))]
    drawn = drawn.at[tuple(spot)].set(least)
    longest = shape.index(max(shape))
    spot[longest] = (spot[longest] + 1) % shape[longest]
    return drawn.at[tuple(spot)].set(high)


def level_of(key, extent, split, least, largest):
    factor_of, own = 1.0, jax.random.fold_in(key, 6)
    for axis_at, blocks in split:
        heights = jnp.exp(jax.random.uniform(jax.random.fold_in(own, axis_at), (blocks,), jnp.float32, least / len(split), largest / len(split)))
        factor_of = factor_of * jnp.repeat(heights, extent[axis_at] // blocks).reshape([-1 if axis == axis_at else 1 for axis in range(len(extent))])
    return factor_of


def centred(own_key, shape, deviation, bound, split=(), held_as=jnp.bfloat16):
    values = deviation * jax.random.normal(own_key, shape, jnp.float32)
    if split:
        values = values * level_of(own_key, shape, split, -0.22, 0.18)
    return jnp.clip(values, -bound, bound).astype(held_as)


def setup_inputs(seed: int = 0) -> dict:
    arg_keys = jax.random.split(jax.random.key(seed), 8)
    e_field = centred(arg_keys[0], (3, NX, NY, NZ), 1.0, 6.0, ((1, 2), (2, 4), (3, 4)), jnp.float32)
    h_field = centred(arg_keys[1], (3, NX, NY, NZ), 1.0, 6.0, ((1, 2), (2, 4), (3, 4)), jnp.float32)
    material = with_ends((jax.random.randint(arg_keys[2], (NX, NY, NZ), 0, 4) < 1).astype(jnp.int32), jax.random.fold_in(arg_keys[2], 1), 0, 1)
    coef_index = with_ends(jax.random.randint(arg_keys[3], (NX, NY, NZ), 0, NTAB), jax.random.fold_in(arg_keys[3], 1), 0, NTAB - 1).astype(jnp.int32)
    table_h = jnp.clip(jnp.exp(jax.random.uniform(arg_keys[4], (NTAB, 3), jnp.float32, math.log(0.15), math.log(0.6))), 0.15, 0.6)
    table_e = jnp.clip(jnp.exp(jax.random.uniform(arg_keys[5], (NTAB, 3), jnp.float32, math.log(0.15), math.log(0.55))), 0.15, 0.55)
    pickup = centred(arg_keys[6], (NZ,), NZ ** -0.5, 0.25, ((0, 4),), jnp.float32)
    return dict(e_field=e_field, h_field=h_field, material=material, coef_index=coef_index, table_h=table_h, table_e=table_e, pickup=pickup)


def next_cells(values, along):
    widths = [(0, 0)] * values.ndim
    widths[along] = (0, 1)
    return lax.slice_in_dim(jnp.pad(values, widths), 1, values.shape[along] + 1, axis=along)


def prior_cells(values, along):
    widths = [(0, 0)] * values.ndim
    widths[along] = (1, 0)
    return lax.slice_in_dim(jnp.pad(values, widths), 0, values.shape[along], axis=along)


def forward_curl(vector):
    primary = (next_cells(vector[2], 1) - vector[2]) - (next_cells(vector[1], 2) - vector[1])
    secondary = (next_cells(vector[0], 2) - vector[0]) - (next_cells(vector[2], 0) - vector[2])
    tertiary = (next_cells(vector[1], 0) - vector[1]) - (next_cells(vector[0], 1) - vector[0])
    return jnp.stack([primary, secondary, tertiary])


def backward_curl(vector):
    primary = (vector[2] - prior_cells(vector[2], 1)) - (vector[1] - prior_cells(vector[1], 2))
    secondary = (vector[0] - prior_cells(vector[0], 2)) - (vector[2] - prior_cells(vector[2], 0))
    tertiary = (vector[1] - prior_cells(vector[1], 0)) - (vector[0] - prior_cells(vector[0], 1))
    return jnp.stack([primary, secondary, tertiary])


def reference(e_field, h_field, material, coef_index, table_h, table_e, pickup):
    magnetic_rate = jnp.moveaxis(table_h[coef_index], 3, 0)
    electric_rate = jnp.moveaxis(table_e[coef_index], 3, 0)
    opened = (1 - material).astype(jnp.float32)
    magnetic = h_field - magnetic_rate * forward_curl(e_field)
    electric = opened * (e_field + electric_rate * backward_curl(magnetic))
    electric_out = next_cells(electric, 3)
    magnetic_out = next_cells(magnetic, 3)
    wake_map = jnp.sum(pickup * electric_out[2], axis=2)
    return electric_out, magnetic_out, wake_map
```

```python
import functools

import jax
import jax.numpy as jnp
from jax import lax
from jax.experimental import pallas as pl
from jax.experimental.pallas import tpu as pltpu
from jax.sharding import PartitionSpec as P

AXES = ("gz", "gx", "gy")
VMEM = pl.BlockSpec(memory_space=pltpu.VMEM)
SMEM = pl.BlockSpec(memory_space=pltpu.SMEM)
ANY = pl.BlockSpec(memory_space=pl.ANY)
LIMIT = 16 * 1024 * 1024


def call(body, outs, in_specs, out_specs=None, scratch=(), cost=1000000):
    return pl.pallas_call(
        body,
        out_shape=outs,
        in_specs=in_specs,
        out_specs=out_specs if out_specs is not None else [VMEM] * len(outs),
        scratch_shapes=scratch,
        compiler_params=pltpu.CompilerParams(vmem_limit_bytes=LIMIT),
        cost_estimate=pl.CostEstimate(flops=cost, bytes_accessed=cost, transcendentals=0),
    )


def f32(*shape):
    return jax.ShapeDtypeStruct(shape, jnp.float32)


def paired(block, axis, first, spare):
    sizes = [lax.axis_size(a) for a in AXES]
    at, other = AXES.index(axis), AXES.index(spare)
    size = sizes[at]
    pairs = []
    for flat in range(sizes[0] * sizes[1] * sizes[2]):
        where = [flat // (sizes[1] * sizes[2]), flat // sizes[2] % sizes[1], flat % sizes[2]]
        up = where[at] % 2 == first
        target = where[at] + (1 if up else -1)
        if 0 <= target < size:
            where[at] = target
        elif sizes[other] % 2 == 0:
            where[other] = where[other] ^ 1
        else:
            continue
        pairs.append((flat, (where[0] * sizes[1] + where[1]) * sizes[2] + where[2]))
    return lax.ppermute(block, AXES, pairs)


def swapped(block, axis, mask):
    return lax.ppermute(block, axis, [(i, i ^ mask) for i in range(lax.axis_size(axis))])


def from_both(first, second, axis):
    index, size = lax.axis_index(axis), lax.axis_size(axis)
    odd = index % 2 == 1

    def previous(*at):
        got = jnp.where(odd, first[at], second[at])
        return jnp.where(index > 0, got, jnp.zeros_like(got))

    def following(*at):
        got = jnp.where(odd, second[at], first[at])
        return jnp.where(index < size - 1, got, jnp.zeros_like(got))

    return previous, following


def lanes(shape):
    return lax.broadcasted_iota(jnp.int32, shape, len(shape) - 1)


def rows(shape):
    return lax.broadcasted_iota(jnp.int32, shape, len(shape) - 2)


def turn(x, amount):
    return pltpu.roll(x, amount % x.shape[-1], axis=x.ndim - 1)


def ahead(x):
    return jnp.where(lanes(x.shape) == x.shape[-1] - 1, 0.0, turn(x, -1))


def behind(x):
    return jnp.where(lanes(x.shape) == 0, 0.0, turn(x, 1))


def upper(x, edge):
    moved = pltpu.roll(x, x.shape[0] - 1, axis=0)
    return jnp.where(rows(x.shape) == x.shape[0] - 1, edge, moved)


def lower(x, edge):
    moved = pltpu.roll(x, 1, axis=0)
    return jnp.where(rows(x.shape) == 0, edge, moved)


def look(table, index):
    return jnp.take_along_axis(table, index, axis=1, mode="promise_in_bounds")


def face_x(e, h, coef, th, te, out_a, out_b, tabs):
    ny, nz = e.shape[2], e.shape[3]
    top = e.shape[1] - 1
    lane = lanes((ny, nz))
    for source, base in ((th, 0), (te, 3)):
        for c in range(3):
            row = jnp.zeros((ny, nz), jnp.float32)
            for n in range(source.shape[0]):
                row = jnp.where(lane == n, source[n, c], row)
            tabs[base + c] = row
    odd = lax.axis_index("gx") % 2 == 1
    index = coef[top]
    ex, ey, ez = e[0, top], e[1, top], e[2, top]
    rate_y, rate_z = look(tabs[1], index), look(tabs[2], index)
    part_y = h[1, top] - rate_y * ((ahead(ex) - ex) + ez)
    part_z = h[2, top] + rate_z * (ey + (upper(ex, 0.0) - ex))
    ups = (part_y, rate_y, part_z, rate_z, ex)
    downs = (e[1, 0], e[2, 0], ex, ex, ex)
    for n, (up, down) in enumerate(zip(ups, downs)):
        out_a[n] = jnp.where(odd, down, up)
        if out_b is not None:
            out_b[n] = jnp.where(odd, up, down)


def face_y(e, h, coef, tabs, xa, xb, out_a, out_b):
    nx, ny = e.shape[1], e.shape[2]
    last = ny - 1
    before_x, after_x = from_both(xa, xb, "gx")
    odd = lax.axis_index("gy") % 2 == 1
    index = coef[:, last, :]
    table_x, table_z = tabs[0, :nx], tabs[2, :nx]
    ex, ey, ez = e[0, :, last, :], e[1, :, last, :], e[2, :, last, :]
    rate_x, rate_z = look(table_x, index), look(table_z, index)
    part_x = h[0, :, last, :] + rate_x * (ez + (ahead(ey) - ey))
    beyond = after_x(0, slice(last, ny))
    next_y = jnp.concatenate([ey[1:], beyond], axis=0)
    part_z = h[2, :, last, :] - rate_z * ((next_y - ey) + ex)
    corner = jnp.broadcast_to(before_x(4, slice(0, 1)), ex.shape)
    ups = (part_x, rate_x, part_z, rate_z, ey)
    downs = (e[0, :, 0, :], e[2, :, 0, :], corner, ey, ey)
    for n, (up, down) in enumerate(zip(ups, downs)):
        out_a[n] = jnp.where(odd, down, up)
        if out_b is not None:
            out_b[n] = jnp.where(odd, up, down)


HY, HX, RX, RY, EZ = range(5)
EX_, EY_, WAKE, AX, AY = range(5)


def place(acc, x, first):
    lane = lanes(x.shape)
    moved = turn(x, first + 1)
    return jnp.where((lane >= first) & (lane <= first + 1), moved, acc)


def interior(e, h, material, coef, tabs, pickup, xa, xb, ya, yb, e_new, h_new, tell, hs):
    nx, ny, nz = e.shape[1], e.shape[2], e.shape[3]
    group = 2 * nx
    before_x, after_x = from_both(xa, xb, "gx")
    before_y, after_y = from_both(ya, yb, "gy")
    plane = (ny, nz)
    lane = lanes(plane)
    first_lane = lane == 0
    th = [tabs[c] for c in range(3)]
    te = [tabs[3 + c] for c in range(3)]
    weight = jnp.broadcast_to(behind(pickup[...]), plane)

    ez0, ey0 = e[2, 0], e[1, 0]
    rate_ym, rate_zm, ex_m = before_x(1), before_x(3), before_x(4)
    corner = after_y(2, slice(0, 1))
    hy_m = before_x(0) + rate_ym * ez0
    hz_m = before_x(2) - rate_zm * ey0
    hz_m = hz_m + jnp.where(rows(plane) == ny - 1, rate_zm * corner, 0.0)
    rate_xn, rate_zn, ey_n = before_y(1), before_y(3), before_y(4)
    hx_n = before_y(0) - rate_xn * e[2, :, 0, :]
    hz_n = before_y(2) + rate_zn * e[0, :, 0, :]
    ex_q, ez_q = after_y(0), after_y(1)

    one = jnp.zeros(plane, jnp.float32)
    two = jnp.where(lane >= nz - 2, jnp.broadcast_to(pickup[...], plane), 0.0)
    two = place(two, jnp.where(first_lane, ex_m, rate_ym), 0)
    for i in range(nx):
        index = coef[i]
        ex, ey, ez = e[0, i], e[1, i], e[2, i]
        if i < nx - 1:
            ey_i, ez_i = e[1, i + 1], e[2, i + 1]
        else:
            ey_i, ez_i = after_x(0), after_x(1)
        rate_x, rate_y, rate_z = [look(t, index) for t in th]
        hx = h[0, i] - rate_x * ((upper(ez, ez_q[i : i + 1]) - ez) - (ahead(ey) - ey))
        hy = h[1, i] - rate_y * ((ahead(ex) - ex) - (ez_i - ez))
        hz = h[2, i] - rate_z * ((ey_i - ey) - (upper(ex, ex_q[i : i + 1]) - ex))
        opened = (1 - material[i]).astype(jnp.float32)
        re_x, re_y, re_z = [opened * look(t, index) for t in te]
        hz_j = lower(hz, hz_n[i : i + 1])
        hx_j = lower(hx, hx_n[i : i + 1])
        ex_new = opened * ex + re_x * ((hz - hz_j) - (hy - behind(hy)))
        ey_new = opened * ey + re_y * ((hx - behind(hx)) - (hz - hz_m))
        ez_new = opened * ez + re_z * ((hy - hy_m) - (hx - hx_j))
        hy_m, hz_m = hy, hz
        for c, value in enumerate((ex_new, ey_new, ez_new)):
            e_new[c, i] = ahead(value)
        for c, value in enumerate((hx, hy, hz)):
            h_new[c, i] = ahead(value)
        wake = jnp.sum(weight * ez_new, axis=1, keepdims=True)
        at = 2 * i
        one = place(one, hy, HY * group + at)
        one = place(one, hx, HX * group + at)
        one = place(one, re_x, RX * group + at)
        one = place(one, re_y, RY * group + at)
        one = place(one, jnp.where(first_lane, ez_new, re_z), EZ * group + at)
        at = at + 2
        two = place(two, jnp.where(first_lane, ex, rate_y), EX_ * group + at)
        two = place(two, jnp.where(first_lane, ey, rate_x), EY_ * group + at)
        two = place(two, jnp.where(first_lane, hz, wake), WAKE * group + at)
        two = place(two, ex_new, AX * group + at)
        two = place(two, ey_new, AY * group + at)
    edge = jnp.zeros((8, nz), jnp.float32)
    pair = jnp.where(lanes(ey_n.shape) == 0, ey_n, rate_xn)
    for i in range(nx):
        edge = place(edge, jnp.broadcast_to(pair[i : i + 1], edge.shape), EY_ * group + 2 + 2 * i)
    tell[0:8, 0:nz] = jnp.zeros((8, nz), jnp.float32)
    tell[0:8, nz:] = edge
    tell[8:, 0:nz] = one
    tell[8:, nz:] = two


def wake_term(mine, beyond, nx):
    nz = mine.shape[-1] // 2
    ny = mine.shape[0] - 8
    group = 2 * nx
    own_one, own_two = mine[8:, :nz], mine[8:, nz:]
    far_one = beyond(slice(8, 8 + ny), slice(0, nz))
    far_two = beyond(slice(8, 8 + ny), slice(nz, 2 * nz))
    far_edge = beyond(slice(7, 7 + ny), slice(nz, 2 * nz))
    product = own_two * turn(far_two, -1)
    product_j = mine[7 : 7 + ny, nz:] * turn(far_edge, -1)
    late_hy = -product
    late_hx = turn(product, -EY_ * group)
    late_hx_j = turn(product_j, -EY_ * group)
    late_ez = turn(own_one, 2 - EZ * group) * ((late_hy - turn(late_hy, 2)) - (late_hx - late_hx_j))
    part = (
        turn(own_two, -WAKE * group)
        + own_two[:, nz - 2 : nz - 1] * late_ez
        + own_two[:, nz - 1 : nz] * turn(far_one, 1 - EZ * group)
    )
    return part, late_hx, late_hy, late_ez, far_one, far_two, own_one


def finish(nx, blocks, e_new, h_new, *refs):
    nz = e_new.shape[-1]
    group = 2 * nx
    tells, (e_out, h_out, wake, e_buf, h_buf, every, flat, sems) = refs[:-8], refs[-8:]
    z, size = lax.axis_index("gz"), lax.axis_size("gz")
    ny = e_new.shape[2]
    own = tells[0]
    if blocks is None:
        inside = z < size - 1
        beyond_ref = tells[1]
        beyond = lambda *at: jnp.where(inside, beyond_ref[at], 0.0)
        part, late_hx, late_hy, late_ez, far_one, far_two, own_one = wake_term(own, beyond, nx)
        total = part
    else:
        for m, ref in enumerate(tells):
            every[z ^ m] = ref[...]
        every[blocks] = jnp.zeros(own.shape, jnp.float32)
        beyond_ref = every.at[z + 1]
        part, late_hx, late_hy, late_ez, far_one, far_two, own_one = wake_term(
            own, lambda *at: beyond_ref[at], nx
        )
    even = lanes((ny, nz)) % 2 == 0
    late_hx_odd, late_hy_odd = turn(late_hx, 1), turn(late_hy, 1)
    hy_last = turn(own_one, 3 - HY * group) + late_hy_odd
    hx_last = turn(own_one, 3 - HX * group) + late_hx_odd
    fix_ex = jnp.where(
        even,
        -turn(own_one, 2 - RX * group) * late_hy,
        turn(far_two, -AX * group) + turn(far_one, 2 - RX * group) * hy_last,
    )
    fix_ey = jnp.where(
        even,
        turn(own_one, 2 - RY * group) * late_hx,
        turn(far_two, -AY * group) - turn(far_one, 2 - RY * group) * hx_last,
    )
    fix_ez = jnp.where(even, late_ez, turn(far_one, 2 - EZ * group))
    fix_hx = jnp.where(even, late_hx, turn(far_one, 2 - HX * group))
    fix_hy = jnp.where(even, late_hy, turn(far_one, 2 - HY * group))
    fix_hz = jnp.where(even, 0.0, turn(far_two, -WAKE * group))
    tail = lanes((ny, nz)) >= nz - 2
    copies = []
    for n, fix in enumerate((fix_ex, fix_ey, fix_ez, fix_hx, fix_hy, fix_hz)):
        source, buf, out = (e_new, e_buf, e_out) if n < 3 else (h_new, h_buf, h_out)
        c = n % 3
        for i in range(nx):
            moved = turn(fix, nz - 4 - 2 * i)
            buf[c, i] = source[c, i] + jnp.where(tail, moved, 0.0)
        copy = pltpu.make_async_copy(buf.at[c], out.at[c], sems.at[n])
        copy.start()
        copies.append(copy)
    if blocks is not None:
        total = None
        for b in range(blocks):
            nearby = every.at[b + 1]
            part = wake_term(every.at[b], lambda *at: nearby[at], nx)[0]
            total = part if total is None else total + part
    flat[...] = total.T
    for i in range(nx):
        wake[i : i + 1, :] = flat[2 + 2 * i : 3 + 2 * i, :]
    for copy in copies:
        copy.wait()


def shards(e_field, h_field, material, coef_index, table_h, table_e, pickup):
    _, nx, ny, nz = e_field.shape
    size_x, size_y, size_z = (lax.axis_size(a) for a in ("gx", "gy", "gz"))
    face = f32(5, ny, nz)
    twice = size_x > 2
    body = face_x if twice else lambda *r: face_x(*r[:-2], r[-2], None, r[-1])
    got = call(body, [face] * (1 + twice) + [f32(6, ny, nz)], [VMEM, VMEM, VMEM, SMEM, SMEM])(
        e_field, h_field, coef_index, table_h, table_e
    )
    tabs = got[-1]
    xa = paired(got[0], "gx", 0, "gy")
    xb = paired(got[1], "gx", 1, "gy") if twice else xa
    edge = f32(5, nx, nz)
    twice = size_y > 2
    body = face_y if twice else lambda *r: face_y(*r, None)
    got = call(body, [edge] * (1 + twice), [VMEM] * 6)(e_field, h_field, coef_index, tabs, xa, xb)
    ya = paired(got[0], "gy", 0, "gx")
    yb = paired(got[1], "gy", 1, "gx") if twice else ya
    whole = f32(3, nx, ny, nz)
    note = f32(ny + 8, 2 * nz)
    e_new, h_new, tell = call(
        interior, [whole, whole, note], [VMEM] * 10, scratch=[pltpu.VMEM((1, ny, nz), jnp.float32)]
    )(e_field, h_field, material, coef_index, tabs, pickup.reshape(1, nz), xa, xb, ya, yb)
    blocks = size_z if size_z in (2, 4) else None
    if blocks:
        tells = [tell] + [swapped(tell, "gz", m) for m in range(1, blocks)]
    else:
        route = [(i, i - 1) for i in range(1, size_z)]
        tells = [tell, lax.ppermute(tell, "gz", route)]
    scratch = [
        pltpu.VMEM((3, nx, ny, nz), jnp.float32),
        pltpu.VMEM((3, nx, ny, nz), jnp.float32),
        pltpu.VMEM(((blocks or 0) + 1, ny + 8, 2 * nz), jnp.float32),
        pltpu.VMEM((nz, ny), jnp.float32),
        pltpu.SemaphoreType.DMA((6,)),
    ]
    e_out, h_out, wake = call(
        functools.partial(finish, nx, blocks),
        [whole, whole, f32(nx, ny)],
        [VMEM] * (2 + len(tells)),
        out_specs=[ANY, ANY, VMEM],
        scratch=scratch,
    )(e_new, h_new, *tells)
    if not blocks:
        wake = lax.psum(wake, "gz")
    return e_out, h_out, wake


def solution(mesh):
    return jax.shard_map(
        shards,
        mesh=mesh,
        in_specs=(
            P(None, "gx", "gy", "gz"),
            P(None, "gx", "gy", "gz"),
            P("gx", "gy", "gz"),
            P("gx", "gy", "gz"),
            P(),
            P(),
            P("gz"),
        ),
        out_specs=(P(None, "gx", "gy", "gz"), P(None, "gx", "gy", "gz"), P("gx", "gy")),
        check_vma=False,
    )
```

```python
import functools

import jax
import jax.numpy as jnp
from jax import lax
from jax.experimental import pallas as pl
from jax.experimental.pallas import tpu as pltpu
from jax.sharding import PartitionSpec as P

AXES = ("gz", "gx", "gy")
VMEM = pl.BlockSpec(memory_space=pltpu.VMEM)
SMEM = pl.BlockSpec(memory_space=pltpu.SMEM)
ANY = pl.BlockSpec(memory_space=pl.ANY)
HBM = pl.BlockSpec(memory_space=pltpu.HBM)
LIMIT = 16 * 1024 * 1024


def call(body, outs, in_specs, out_specs=None, scratch=(), cost=1000000):
    return pl.pallas_call(
        body,
        out_shape=outs,
        in_specs=in_specs,
        out_specs=out_specs if out_specs is not None else [VMEM] * len(outs),
        scratch_shapes=scratch,
        compiler_params=pltpu.CompilerParams(vmem_limit_bytes=LIMIT),
        cost_estimate=pl.CostEstimate(flops=cost, bytes_accessed=cost, transcendentals=0),
    )


def stay(x):
    return pltpu.with_memory_space_constraint(x, pltpu.HBM)


def f32(*shape):
    return jax.ShapeDtypeStruct(shape, jnp.float32)


def paired(block, axis, first, spare):
    sizes = [lax.axis_size(a) for a in AXES]
    at, other = AXES.index(axis), AXES.index(spare)
    size = sizes[at]
    pairs = []
    for flat in range(sizes[0] * sizes[1] * sizes[2]):
        where = [flat // (sizes[1] * sizes[2]), flat // sizes[2] % sizes[1], flat % sizes[2]]
        up = where[at] % 2 == first
        target = where[at] + (1 if up else -1)
        if 0 <= target < size:
            where[at] = target
        elif sizes[other] % 2 == 0:
            where[other] = where[other] ^ 1
        else:
            continue
        pairs.append((flat, (where[0] * sizes[1] + where[1]) * sizes[2] + where[2]))
    return lax.ppermute(block, AXES, pairs)


def swapped(block, axis, mask):
    return lax.ppermute(block, axis, [(i, i ^ mask) for i in range(lax.axis_size(axis))])


def from_both(first, second, axis):
    index, size = lax.axis_index(axis), lax.axis_size(axis)
    odd = index % 2 == 1

    def previous(*at):
        got = jnp.where(odd, first[at], second[at])
        return jnp.where(index > 0, got, jnp.zeros_like(got))

    def following(*at):
        got = jnp.where(odd, second[at], first[at])
        return jnp.where(index < size - 1, got, jnp.zeros_like(got))

    return previous, following


def lanes(shape):
    return lax.broadcasted_iota(jnp.int32, shape, len(shape) - 1)


def rows(shape):
    return lax.broadcasted_iota(jnp.int32, shape, len(shape) - 2)


def turn(x, amount):
    return pltpu.roll(x, amount % x.shape[-1], axis=x.ndim - 1)


def ahead(x):
    return jnp.where(lanes(x.shape) == x.shape[-1] - 1, 0.0, turn(x, -1))


def behind(x):
    return jnp.where(lanes(x.shape) == 0, 0.0, turn(x, 1))


def upper(x, edge):
    moved = pltpu.roll(x, x.shape[0] - 1, axis=0)
    return jnp.where(rows(x.shape) == x.shape[0] - 1, edge, moved)


def lower(x, edge):
    moved = pltpu.roll(x, 1, axis=0)
    return jnp.where(rows(x.shape) == 0, edge, moved)


def look(table, index):
    return jnp.take_along_axis(table, index, axis=1, mode="promise_in_bounds")


def face_x(e, h, coef, th, te, out_a, out_b, tabs, eb, hb, cb, tb, sems):
    ny, nz = e.shape[2], e.shape[3]
    top = e.shape[1] - 1
    moves = [
        (e.at[:, top], eb.at[0:3]),
        (e.at[1:3, 0], eb.at[3:5]),
        (h.at[1:3, top], hb),
        (coef.at[top], cb),
        (th, tb.at[0]),
        (te, tb.at[1]),
    ]
    copies = [pltpu.make_async_copy(a, b, sems.at[n]) for n, (a, b) in enumerate(moves)]
    for copy in copies:
        copy.start()
    for copy in copies:
        copy.wait()
    entries = th.shape[1]
    for base in range(2):
        for c in range(3):
            row = jnp.broadcast_to(tb[base, c : c + 1, :], (ny, entries))
            tabs[3 * base + c] = jnp.concatenate([row, jnp.zeros((ny, nz - entries), jnp.float32)], axis=1)
    odd = lax.axis_index("gx") % 2 == 1
    index = cb[...]
    ex, ey, ez = eb[0], eb[1], eb[2]
    rate_y, rate_z = look(tabs[1], index), look(tabs[2], index)
    part_y = hb[0] - rate_y * ((ahead(ex) - ex) + ez)
    part_z = hb[1] + rate_z * (ey + (upper(ex, 0.0) - ex))
    ups = (part_y, rate_y, part_z, rate_z, ex)
    downs = (eb[3], eb[4], ex, ex, ex)
    for n, (up, down) in enumerate(zip(ups, downs)):
        out_a[n] = jnp.where(odd, down, up)
        if out_b is not None:
            out_b[n] = jnp.where(odd, up, down)


def face_y(e, h, rate, xa, xb, out_a, out_b):
    nx, ny = e.shape[1], e.shape[2]
    last = ny - 1
    before_x, after_x = from_both(xa, xb, "gx")
    odd = lax.axis_index("gy") % 2 == 1
    ex, ey, ez = e[0, :, last, :], e[1, :, last, :], e[2, :, last, :]
    rate_x, rate_z = rate[0, :, last, :], rate[2, :, last, :]
    part_x = h[0, :, last, :] + rate_x * (ez + (ahead(ey) - ey))
    beyond = after_x(0, slice(last, ny))
    next_y = jnp.concatenate([ey[1:], beyond], axis=0)
    part_z = h[2, :, last, :] - rate_z * ((next_y - ey) + ex)
    corner = jnp.broadcast_to(before_x(4, slice(0, 1)), ex.shape)
    ups = (part_x, rate_x, part_z, rate_z, ey)
    downs = (e[0, :, 0, :], e[2, :, 0, :], corner, ey, ey)
    for n, (up, down) in enumerate(zip(ups, downs)):
        out_a[n] = jnp.where(odd, down, up)
        if out_b is not None:
            out_b[n] = jnp.where(odd, up, down)


HY, HX, RX, RY, EZ = range(5)
EX_, EY_, WAKE, AX, AY = range(5)


def place(acc, x, first):
    lane = lanes(x.shape)
    moved = turn(x, first + 1)
    return jnp.where((lane >= first) & (lane <= first + 1), moved, acc)


def rates(e, material, coef, tabs, rate, pack):
    nx, ny, nz = e.shape[1], e.shape[2], e.shape[3]
    group = 2 * nx
    plane = (ny, nz)
    first_lane = lanes(plane) == 0
    one = jnp.zeros(plane, jnp.float32)
    two = jnp.zeros(plane, jnp.float32)
    for i in range(nx):
        index = coef[i]
        opened = (1 - material[i]).astype(jnp.float32)
        rh = [look(tabs[c], index) for c in range(3)]
        re = [opened * look(tabs[3 + c], index) for c in range(3)]
        for c in range(3):
            rate[c, i] = rh[c]
            rate[3 + c, i] = re[c]
        at = 2 * i
        one = place(one, re[0], RX * group + at)
        one = place(one, re[1], RY * group + at)
        one = place(one, re[2], EZ * group + at)
        at = at + 2
        two = place(two, jnp.where(first_lane, e[0, i], rh[1]), EX_ * group + at)
        two = place(two, jnp.where(first_lane, e[1, i], rh[0]), EY_ * group + at)
        two = place(two, opened, AX * group + at)
        two = place(two, e[2, i], AY * group + at)
    pack[0] = one
    pack[1] = two


def interior(e, h, material, rate, pack, pickup, xa, xb, field, below, out):
    nx, ny, nz = e.shape[1], e.shape[2], e.shape[3]
    group = 2 * nx
    before_x, after_x = from_both(xa, xb, "gx")
    plane = (ny, nz)
    lane = lanes(plane)
    first_lane = lane == 0
    weight = jnp.broadcast_to(behind(pickup[...]), plane)
    hy_m = before_x(0) + before_x(1) * e[2, 0]
    hz_m = before_x(2) - before_x(3) * e[1, 0]
    below[0] = hy_m
    below[1] = hz_m
    one = pack[0]
    two = jnp.where(lane >= nz - 2, jnp.broadcast_to(pickup[...], plane), pack[1])
    two = place(two, jnp.where(first_lane, before_x(4), before_x(1)), 0)
    for i in range(nx):
        ex, ey, ez = e[0, i], e[1, i], e[2, i]
        if i < nx - 1:
            ey_i, ez_i = e[1, i + 1], e[2, i + 1]
        else:
            ey_i, ez_i = after_x(0), after_x(1)
        hx = h[0, i] - rate[0, i] * ((upper(ez, 0.0) - ez) - (ahead(ey) - ey))
        hy = h[1, i] - rate[1, i] * ((ahead(ex) - ex) - (ez_i - ez))
        hz = h[2, i] - rate[2, i] * ((ey_i - ey) - (upper(ex, 0.0) - ex))
        field[0, i] = hx
        field[1, i] = hy
        field[2, i] = hz
        opened = (1 - material[i]).astype(jnp.float32)
        ez_new = opened * ez + rate[5, i] * ((hy - hy_m) - (hx - lower(hx, 0.0)))
        hy_m = hy
        wake = jnp.sum(weight * ez_new, axis=1, keepdims=True)
        one = place(one, hy, HY * group + 2 * i)
        one = place(one, hx, HX * group + 2 * i)
        two = place(two, jnp.where(first_lane, hz, wake), WAKE * group + 2 + 2 * i)
    out[0] = one
    out[1] = two


def spread(x, first):
    n, nz = x.shape
    full = -(-n // 8) * 8
    if full > n:
        x = jnp.concatenate([x, jnp.zeros((full - n, nz), x.dtype)], axis=0)
    moved = pltpu.roll(x, (first + 1) % nz, axis=1, stride=2, stride_axis=0)
    off = lanes(x.shape) - first - 2 * rows(x.shape)
    row = rows(x.shape)
    keep = (off >= 0) & (off < 2) & (row < n)
    return jnp.sum(jnp.where(keep, moved, 0.0), axis=0, keepdims=True)


def border(e, rate, field, below, pack, pickup, xa, xb, ya, yb, tell, fixed):
    nx, ny, nz = e.shape[1], e.shape[2], e.shape[3]
    group = 2 * nx
    last = ny - 1
    before_x, _ = from_both(xa, xb, "gx")
    before_y, after_y = from_both(ya, yb, "gy")
    plane = (ny, nz)
    lane, row = lanes(plane), rows(plane)
    odd = lane % 2 == 1
    rate_xn, ey_n = before_y(1), before_y(4)
    hx_n = before_y(0) - rate_xn * e[2, :, 0, :]
    hz_n = before_y(2) + before_y(3) * e[0, :, 0, :]
    late_x = rate[0, :, last, :] * after_y(1)
    hx_top = field[0, :, last, :] - late_x
    hz_top = field[2, :, last, :] + rate[2, :, last, :] * after_y(0)
    corner = before_x(3, slice(last, ny)) * after_y(2, slice(0, 1))
    fixed[0] = hx_n
    fixed[1] = hz_n
    fixed[2] = hx_top
    fixed[3] = hz_top
    fixed[4, 0:1] = corner
    weight = jnp.broadcast_to(behind(pickup[...]), hx_n.shape)
    wake_low = jnp.sum(weight * rate[5, :, 0, :] * hx_n, axis=1, keepdims=True)
    wake_top = jnp.sum(weight * rate[5, :, last, :] * late_x, axis=1, keepdims=True)
    firsts = lanes(hx_n.shape) == 0
    at_wake = WAKE * group + 2
    add_low = spread(jnp.where(firsts, 0.0, wake_low), at_wake)
    add_top = spread(jnp.where(firsts, hz_top - field[2, :, last, :], wake_top), at_wake)
    add_hx = spread(-late_x, HX * group)
    one, two = pack[0], pack[1]
    is_top = row == last
    one = one + jnp.where(is_top, add_hx, 0.0)
    two = two + jnp.where(is_top, add_top, jnp.where(row == 0, add_low, 0.0))
    low_hx, low_hz = spread(hx_n, 2), spread(hz_n, 2)
    hy_m = turn(below[0], 3)
    hz_m = turn(below[1] + jnp.where(is_top, corner, 0.0), 3)
    hy = turn(one, 2 - HY * group)
    hx = turn(one, 2 - HX * group)
    hz = turn(two, -WAKE * group)
    opened = turn(two, -AX * group)
    hy_i = jnp.where(lane == 3, hy_m, turn(hy, 2))
    hz_i = jnp.where(lane == 3, hz_m, turn(hz, 2))
    hx_j, hz_j = lower(hx, low_hx), lower(hz, low_hz)
    ex_new = opened * two + turn(one, 2 - RX * group) * ((hz - hz_j) - hy)
    ey_new = opened * turn(two, -EY_ * group) + turn(one, 2 - RY * group) * (hx - (hz - hz_i))
    ez_new = opened * turn(two, -AY * group) + turn(one, 2 - EZ * group) * ((hy - hy_i) - (hx - hx_j))
    inside = lambda g, start: odd & (lane >= g * group + start) & (lane < (g + 1) * group + start)
    one = jnp.where(inside(EZ, 0), turn(ez_new, EZ * group - 2), one)
    two = jnp.where(inside(AX, 2), turn(ex_new, AX * group), two)
    two = jnp.where(inside(AY, 2), turn(ey_new, AY * group), two)
    edge = spread(jnp.where(firsts, ey_n, rate_xn), EY_ * group + 2)
    tell[0:8, 0:nz] = jnp.zeros((8, nz), jnp.float32)
    tell[0:8, nz:] = jnp.broadcast_to(edge, (8, nz))
    tell[8:, 0:nz] = one
    tell[8:, nz:] = two


def outputs(e, material, rate, field, below, fixed, e_new, h_new):
    nx, ny, nz = e.shape[1], e.shape[2], e.shape[3]
    plane = (ny, nz)
    is_top = rows(plane) == ny - 1
    hy_m = below[0]
    hz_m = below[1] + jnp.where(is_top, fixed[4, 0:1], 0.0)
    for i in range(nx):
        hx = jnp.where(is_top, fixed[2, i : i + 1], field[0, i])
        hy = field[1, i]
        hz = jnp.where(is_top, fixed[3, i : i + 1], field[2, i])
        opened = (1 - material[i]).astype(jnp.float32)
        hz_j = lower(hz, fixed[1, i : i + 1])
        hx_j = lower(hx, fixed[0, i : i + 1])
        ex_new = opened * e[0, i] + rate[3, i] * ((hz - hz_j) - (hy - behind(hy)))
        ey_new = opened * e[1, i] + rate[4, i] * ((hx - behind(hx)) - (hz - hz_m))
        ez_new = opened * e[2, i] + rate[5, i] * ((hy - hy_m) - (hx - hx_j))
        hy_m, hz_m = hy, hz
        for c, value in enumerate((ex_new, ey_new, ez_new)):
            e_new[c, i] = ahead(value)
        for c, value in enumerate((hx, hy, hz)):
            h_new[c, i] = ahead(value)


def wake_term(mine, beyond, nx):
    nz = mine.shape[-1] // 2
    ny = mine.shape[0] - 8
    group = 2 * nx
    own_one, own_two = mine[8:, :nz], mine[8:, nz:]
    far_one = beyond(slice(8, 8 + ny), slice(0, nz))
    far_two = beyond(slice(8, 8 + ny), slice(nz, 2 * nz))
    far_edge = beyond(slice(7, 7 + ny), slice(nz, 2 * nz))
    product = own_two * turn(far_two, -1)
    product_j = mine[7 : 7 + ny, nz:] * turn(far_edge, -1)
    late_hy = -product
    late_hx = turn(product, -EY_ * group)
    late_hx_j = turn(product_j, -EY_ * group)
    late_ez = turn(own_one, 2 - EZ * group) * ((late_hy - turn(late_hy, 2)) - (late_hx - late_hx_j))
    part = (
        turn(own_two, -WAKE * group)
        + own_two[:, nz - 2 : nz - 1] * late_ez
        + own_two[:, nz - 1 : nz] * turn(far_one, 1 - EZ * group)
    )
    return part, late_hx, late_hy, late_ez, far_one, far_two, own_one


def finish(nx, blocks, e_new, h_new, *refs):
    nz = e_new.shape[-1]
    group = 2 * nx
    tells, (e_out, h_out, wake, e_buf, h_buf, every, flat, sems) = refs[:-8], refs[-8:]
    z, size = lax.axis_index("gz"), lax.axis_size("gz")
    ny = e_new.shape[2]
    own = tells[0]
    if blocks is None:
        inside = z < size - 1
        beyond_ref = tells[1]
        beyond = lambda *at: jnp.where(inside, beyond_ref[at], 0.0)
        part, late_hx, late_hy, late_ez, far_one, far_two, own_one = wake_term(own, beyond, nx)
        total = part
    else:
        for m, ref in enumerate(tells):
            every[z ^ m] = ref[...]
        every[blocks] = jnp.zeros(own.shape, jnp.float32)
        beyond_ref = every.at[z + 1]
        part, late_hx, late_hy, late_ez, far_one, far_two, own_one = wake_term(
            own, lambda *at: beyond_ref[at], nx
        )
    even = lanes((ny, nz)) % 2 == 0
    late_hx_odd, late_hy_odd = turn(late_hx, 1), turn(late_hy, 1)
    hy_last = turn(own_one, 3 - HY * group) + late_hy_odd
    hx_last = turn(own_one, 3 - HX * group) + late_hx_odd
    fix_ex = jnp.where(
        even,
        -turn(own_one, 2 - RX * group) * late_hy,
        turn(far_two, -AX * group) + turn(far_one, 2 - RX * group) * hy_last,
    )
    fix_ey = jnp.where(
        even,
        turn(own_one, 2 - RY * group) * late_hx,
        turn(far_two, -AY * group) - turn(far_one, 2 - RY * group) * hx_last,
    )
    fix_ez = jnp.where(even, late_ez, turn(far_one, 2 - EZ * group))
    fix_hx = jnp.where(even, late_hx, turn(far_one, 2 - HX * group))
    fix_hy = jnp.where(even, late_hy, turn(far_one, 2 - HY * group))
    fix_hz = jnp.where(even, 0.0, turn(far_two, -WAKE * group))
    tail = lanes((ny, nz)) >= nz - 2
    copies = []
    for n, fix in enumerate((fix_ex, fix_ey, fix_ez, fix_hx, fix_hy, fix_hz)):
        source, buf, out = (e_new, e_buf, e_out) if n < 3 else (h_new, h_buf, h_out)
        c = n % 3
        for i in range(nx):
            moved = turn(fix, nz - 4 - 2 * i)
            buf[c, i] = source[c, i] + jnp.where(tail, moved, 0.0)
        copy = pltpu.make_async_copy(buf.at[c], out.at[c], sems.at[n])
        copy.start()
        copies.append(copy)
    if blocks is not None:
        total = None
        for b in range(blocks):
            nearby = every.at[b + 1]
            part = wake_term(every.at[b], lambda *at: nearby[at], nx)[0]
            total = part if total is None else total + part
    flat[...] = total.T
    for i in range(nx):
        wake[i : i + 1, :] = flat[2 + 2 * i : 3 + 2 * i, :]
    for copy in copies:
        copy.wait()


def shards(e_field, h_field, material, coef_index, table_h, table_e, pickup):
    _, nx, ny, nz = e_field.shape
    size_x, size_y, size_z = (lax.axis_size(a) for a in ("gx", "gy", "gz"))
    face = f32(5, ny, nz)
    twice = size_x > 2
    body = face_x if twice else lambda *r: face_x(*r[:6], None, *r[6:])
    buffers = [
        pltpu.VMEM((5, ny, nz), jnp.float32),
        pltpu.VMEM((2, ny, nz), jnp.float32),
        pltpu.VMEM((ny, nz), jnp.int32),
        pltpu.VMEM((2, 3, table_h.shape[0]), jnp.float32),
        pltpu.SemaphoreType.DMA((6,)),
    ]
    got = call(body, [face] * (1 + twice) + [f32(6, ny, nz)], [HBM] * 5, scratch=buffers)(
        *(stay(x) for x in (e_field, h_field, coef_index, table_h.T, table_e.T))
    )
    tabs = got[-1]
    xa = paired(got[0], "gx", 0, "gy")
    xb = paired(got[1], "gx", 1, "gy") if twice else xa
    whole = f32(3, nx, ny, nz)
    pair = f32(2, ny, nz)
    rate, pack = call(rates, [f32(6, nx, ny, nz), pair], [VMEM] * 4)(e_field, material, coef_index, tabs)
    edge = f32(5, nx, nz)
    twice = size_y > 2
    body = face_y if twice else lambda *r: face_y(*r, None)
    got = call(body, [edge] * (1 + twice), [VMEM] * 5)(e_field, h_field, rate, xa, xb)
    ya = paired(got[0], "gy", 0, "gx")
    yb = paired(got[1], "gy", 1, "gx") if twice else ya
    weights = pickup.reshape(1, nz)
    field, below, pack = call(interior, [whole, pair, pair], [VMEM] * 8)(
        e_field, h_field, material, rate, pack, weights, xa, xb
    )
    note = f32(ny + 8, 2 * nz)
    tell, fixed = call(border, [note, edge], [VMEM] * 10)(
        e_field, rate, field, below, pack, weights, xa, xb, ya, yb
    )
    e_new, h_new = call(outputs, [whole, whole], [VMEM] * 6)(
        e_field, material, rate, field, below, fixed
    )
    blocks = size_z if size_z in (2, 4) else None
    if blocks:
        tells = [tell] + [swapped(tell, "gz", m) for m in range(1, blocks)]
    else:
        route = [(i, i - 1) for i in range(1, size_z)]
        tells = [tell, lax.ppermute(tell, "gz", route)]
    scratch = [
        pltpu.VMEM((3, nx, ny, nz), jnp.float32),
        pltpu.VMEM((3, nx, ny, nz), jnp.float32),
        pltpu.VMEM(((blocks or 0) + 1, ny + 8, 2 * nz), jnp.float32),
        pltpu.VMEM((nz, ny), jnp.float32),
        pltpu.SemaphoreType.DMA((6,)),
    ]
    e_out, h_out, wake = call(
        functools.partial(finish, nx, blocks),
        [whole, whole, f32(nx, ny)],
        [VMEM] * (2 + len(tells)),
        out_specs=[ANY, ANY, VMEM],
        scratch=scratch,
    )(e_new, h_new, *tells)
    if not blocks:
        wake = lax.psum(wake, "gz")
    return e_out, h_out, wake


def solution(mesh):
    return jax.shard_map(
        shards,
        mesh=mesh,
        in_specs=(
            P(None, "gx", "gy", "gz"),
            P(None, "gx", "gy", "gz"),
            P("gx", "gy", "gz"),
            P("gx", "gy", "gz"),
            P(),
            P(),
            P("gz"),
        ),
        out_specs=(P(None, "gx", "gy", "gz"), P(None, "gx", "gy", "gz"), P("gx", "gy")),
        check_vma=False,
    )
```

```python
import functools

import jax
import jax.numpy as jnp
from jax import lax
from jax.experimental import pallas as pl
from jax.experimental.pallas import tpu as pltpu
from jax.sharding import PartitionSpec as P

AXES = ("gz", "gx", "gy")
VMEM = pl.BlockSpec(memory_space=pltpu.VMEM)
SMEM = pl.BlockSpec(memory_space=pltpu.SMEM)
ANY = pl.BlockSpec(memory_space=pl.ANY)
HBM = pl.BlockSpec(memory_space=pltpu.HBM)
LIMIT = 16 * 1024 * 1024


def call(body, outs, in_specs, out_specs=None, scratch=(), cost=1000000):
    return pl.pallas_call(
        body,
        out_shape=outs,
        in_specs=in_specs,
        out_specs=out_specs if out_specs is not None else [VMEM] * len(outs),
        scratch_shapes=scratch,
        compiler_params=pltpu.CompilerParams(vmem_limit_bytes=LIMIT),
        cost_estimate=pl.CostEstimate(flops=cost, bytes_accessed=cost, transcendentals=0),
    )


def stay(x):
    return pltpu.with_memory_space_constraint(x, pltpu.HBM)


def f32(*shape):
    return jax.ShapeDtypeStruct(shape, jnp.float32)


def paired(block, axis, first, spare):
    sizes = [lax.axis_size(a) for a in AXES]
    at, other = AXES.index(axis), AXES.index(spare)
    size = sizes[at]
    pairs = []
    for flat in range(sizes[0] * sizes[1] * sizes[2]):
        where = [flat // (sizes[1] * sizes[2]), flat // sizes[2] % sizes[1], flat % sizes[2]]
        up = where[at] % 2 == first
        target = where[at] + (1 if up else -1)
        if 0 <= target < size:
            where[at] = target
        elif sizes[other] % 2 == 0:
            where[other] = where[other] ^ 1
        else:
            continue
        pairs.append((flat, (where[0] * sizes[1] + where[1]) * sizes[2] + where[2]))
    return lax.ppermute(block, AXES, pairs)


def swapped(block, axis, mask):
    return lax.ppermute(block, axis, [(i, i ^ mask) for i in range(lax.axis_size(axis))])


def from_both(first, second, axis):
    index, size = lax.axis_index(axis), lax.axis_size(axis)
    odd = index % 2 == 1
    is_previous, is_next = index > 0, index < size - 1

    def previous(start, stop):
        got = jnp.where(odd, first[start:stop], second[start:stop])
        return jnp.where(is_previous, got, 0.0)

    def following(start, stop):
        got = jnp.where(odd, second[start:stop], first[start:stop])
        return jnp.where(is_next, got, 0.0)

    return previous, following, is_previous


def lanes(shape):
    return lax.broadcasted_iota(jnp.int32, shape, len(shape) - 1)


def rows(shape):
    return lax.broadcasted_iota(jnp.int32, shape, len(shape) - 2)


def turn(x, amount):
    if isinstance(amount, int):
        amount = amount % x.shape[-1]
    return pltpu.roll(x, amount, axis=x.ndim - 1)


def ahead(x):
    return jnp.where(lanes(x.shape) == x.shape[-1] - 1, 0.0, turn(x, -1))


def behind(x):
    return jnp.where(lanes(x.shape) == 0, 0.0, turn(x, 1))


def upper(x, edge):
    moved = pltpu.roll(x, x.shape[0] - 1, axis=0)
    return jnp.where(rows(x.shape) == x.shape[0] - 1, edge, moved)


def lower(x, edge):
    moved = pltpu.roll(x, 1, axis=0)
    return jnp.where(rows(x.shape) == 0, edge, moved)


def look(table, index):
    return jnp.take_along_axis(table, index, axis=1, mode="promise_in_bounds")


def send(odd, out_a, out_b, start, up, down):
    stop = start + up.shape[0]
    out_a[start:stop] = jnp.where(odd, down, up)
    if out_b is not None:
        out_b[start:stop] = jnp.where(odd, up, down)


def face_x(e, h, coef, th, te, pickup, out_a, out_b, tabs, eb, hb, cb, tb, pb, sems):
    ny, nz = e.shape[2], e.shape[3]
    top = e.shape[1] - 1
    moves = [
        (e.at[:, top], eb.at[0:3]),
        (coef.at[top], cb),
        (th, tb.at[0]),
        (h.at[1:3, top], hb),
        (e.at[1:3, 0], eb.at[3:5]),
        (te, tb.at[1]),
        (pickup, pb),
    ]
    copies = [pltpu.make_async_copy(a, b, sems.at[n]) for n, (a, b) in enumerate(moves)]
    for copy in copies:
        copy.start()
    for copy in copies:
        copy.wait()
    entries = th.shape[1]
    for base in range(2):
        for c in range(3):
            row = jnp.broadcast_to(tb[base, c : c + 1, :], (ny, entries))
            row = jnp.concatenate([row, jnp.zeros((ny, nz - entries), jnp.float32)], axis=1)
            tabs[3 * base + c] = row + turn(row, entries) if base == 0 else row
    tabs[6] = jnp.broadcast_to(pb[...], (ny, nz))
    odd = lax.axis_index("gx") % 2 == 1
    index = cb[...]
    ex, ey, ez = eb[0], eb[1], eb[2]
    part_y = hb[0] - look(tabs[1], index) * ((ahead(ex) - ex) + ez)
    part_z = hb[1] + look(tabs[2], index) * (ey + (upper(ex, 0.0) - ex))
    column = jnp.where(lanes(ex.shape) == rows(ex.shape), ex[:, 0:1], 0.0)
    column = jnp.sum(column, axis=0, keepdims=True)
    key = index.astype(jnp.float32)
    send(odd, out_a, out_b, 0, part_y, eb[3])
    send(odd, out_a, out_b, ny, part_z, eb[4])
    send(odd, out_a, out_b, 2 * ny, key, key)
    send(odd, out_a, out_b, 3 * ny, ex[0:1], ex[0:1])
    send(odd, out_a, out_b, 3 * ny + 1, column, column)


def face_y(e, h, tabs, index, rate, xa, xb, out_a, out_b):
    nx, ny = e.shape[1], e.shape[2]
    last = ny - 1
    before_x, after_x, _ = from_both(xa, xb, "gx")
    odd = lax.axis_index("gy") % 2 == 1
    key = index[:, last, :]
    ex, ey, ez = e[0, :, last, :], e[1, :, last, :], e[2, :, last, :]
    part_x = h[0, :, last, :] + rate[0, :, last, :] * (ez + (ahead(ey) - ey))
    next_y = jnp.concatenate([ey[1:], after_x(last, ny)], axis=0)
    part_z = h[2, :, last, :] - look(tabs[2, :nx], key) * ((next_y - ey) + ex)
    key = key.astype(jnp.float32)
    send(odd, out_a, out_b, 0, part_x, e[0, :, 0, :])
    send(odd, out_a, out_b, nx, part_z, e[2, :, 0, :])
    send(odd, out_a, out_b, 2 * nx, key, key)
    corner = before_x(3 * ny, 3 * ny + 1)
    send(odd, out_a, out_b, 3 * nx, spread(ey, 0), corner)


def spread(x, first):
    n, nz = x.shape
    full = -(-n // 8) * 8
    if full > n:
        x = jnp.concatenate([x, jnp.zeros((full - n, nz), x.dtype)], axis=0)
    moved = pltpu.roll(x, (first + 1) % nz, axis=1, stride=2, stride_axis=0)
    off = lanes(x.shape) - first - 2 * rows(x.shape)
    row = rows(x.shape)
    keep = (off >= 0) & (off < 2) & (row < n)
    return jnp.sum(jnp.where(keep, moved, 0.0), axis=0, keepdims=True)


HEAD = 8


def place(acc, x, first):
    lane = lanes(x.shape)
    moved = turn(x, first + 1)
    return jnp.where((lane >= first) & (lane <= first + 1), moved, acc)


def joined(parts, group):
    lane = lanes(parts[0].shape)
    acc = parts[0]
    for n, part in enumerate(parts[1:], 1):
        acc = jnp.where(lane >= n * group, turn(part, n * group), acc)
    return acc


def rates(entries, e, material, coef, tabs, index, rate, pack):
    nx, ny, nz = e.shape[1], e.shape[2], e.shape[3]
    plane = (ny, nz)
    first_lane = lanes(plane) == 0
    keys = jnp.zeros(plane, jnp.int32)
    exy = jnp.zeros(plane, jnp.float32)

    def step(i, carry):
        keys, exy = carry
        key = coef[i] + entries * material[i]
        index[i] = key
        for n, c in enumerate((0, 1, 5)):
            rate[n, i] = look(tabs[c], key)
        keys = place(keys, key, 2 * i)
        exy = place(exy, jnp.where(first_lane, e[0, i], turn(e[1, i], -1)), 2 * i)
        return keys, exy

    keys, exy = lax.fori_loop(0, nx, step, (keys, exy), unroll=3)
    pack[0] = exy
    for c in range(6):
        pack[1 + c] = look(tabs[c], keys)
    pack[7] = jnp.where(keys < entries, 1.0, 0.0)


def interior(entries, e, h, rate, index, tabs, xa, xb, hx_out, hy_out, below, own):
    nx, ny, nz = e.shape[1], e.shape[2], e.shape[3]
    before_x, after_x, is_before = from_both(xa, xb, "gx")
    plane = (ny, nz)
    first_lane = lanes(plane) == 0
    weight = behind(tabs[6])
    key = before_x(2 * ny, 3 * ny).astype(jnp.int32)
    rate_ym = jnp.where(is_before, look(tabs[1], key), 0.0)
    rate_zm = jnp.where(is_before, look(tabs[2], key), 0.0)
    hy_m = before_x(0, ny) + rate_ym * e[2, 0]
    below[0] = hy_m
    below[1] = before_x(ny, 2 * ny) - rate_zm * e[1, 0]
    below[2] = rate_ym
    below[3] = rate_zm
    ez_last = after_x(ny, 2 * ny)
    wakes = hz = hx_pair = hy_pair = jnp.zeros(plane, jnp.float32)

    def step(i, carry):
        hy_m, wakes, hz, hx_pair, hy_pair = carry
        ex, ey, ez = e[0, i], e[1, i], e[2, i]
        ez_i = jnp.where(i == nx - 1, ez_last, e[2, jnp.minimum(i + 1, nx - 1)])
        hx = h[0, i] - rate[0, i] * ((upper(ez, 0.0) - ez) - (ahead(ey) - ey))
        hy = h[1, i] - rate[1, i] * ((ahead(ex) - ex) - (ez_i - ez))
        hx_out[i] = hx
        hy_out[i] = hy
        ez_new = ez + rate[2, i] * ((hy - hy_m) - (hx - lower(hx, 0.0)))
        wake = jnp.sum(jnp.where(index[i] < entries, weight * ez_new, 0.0), axis=1, keepdims=True)
        wakes = place(wakes, jnp.where(first_lane, ez, wake), 2 * i)
        hz = place(hz, h[2, i], 2 * i)
        hx_pair = place(hx_pair, hx, 2 * i)
        hy_pair = place(hy_pair, hy, 2 * i)
        return hy, wakes, hz, hx_pair, hy_pair

    carry = (hy_m, wakes, hz, hx_pair, hy_pair)
    _, wakes, hz, hx_pair, hy_pair = lax.fori_loop(0, nx, step, carry, unroll=4)
    own[2] = hx_pair
    own[3] = hz
    own[0] = wakes
    own[1] = hy_pair


def border(e, rate, field, below, pack, own, tabs, xa, xb, ya, yb, near, far, mine, fixed):
    nx, ny, nz = e.shape[1], e.shape[2], e.shape[3]
    group = 2 * nx
    last = ny - 1
    before_x, after_x, _ = from_both(xa, xb, "gx")
    before_y, after_y, is_before = from_both(ya, yb, "gy")
    plane = (ny, nz)
    lane, row = lanes(plane), rows(plane)
    even, is_top = lane % 2 == 0, row == last
    key = before_y(2 * nx, 3 * nx).astype(jnp.int32)
    rate_xn = jnp.where(is_before, look(tabs[0, :nx], key), 0.0)
    rate_zn = jnp.where(is_before, look(tabs[2, :nx], key), 0.0)
    hx_n = before_y(0, nx) - rate_xn * e[2, :, 0, :]
    hz_n = before_y(nx, 2 * nx) + rate_zn * e[0, :, 0, :]
    ex_q = after_y(0, nx)
    late_x = rate[0, :, last, :] * after_y(nx, 2 * nx)
    corner = below[3, last:ny] * after_y(3 * nx, 3 * nx + 1)
    fixed[0] = hx_n
    fixed[1] = hz_n
    fixed[2] = field[:, last, :] - late_x
    fixed[3, 0:1] = corner
    weight = behind(tabs[6, :nx])
    wake_low = jnp.sum(weight * rate[2, :, 0, :] * hx_n, axis=1, keepdims=True)
    wake_top = jnp.sum(weight * rate[2, :, last, :] * late_x, axis=1, keepdims=True)
    firsts = lanes(hx_n.shape) == 0
    wakes = own[0] + jnp.where(
        is_top,
        spread(jnp.where(firsts, 0.0, wake_top), 0),
        jnp.where(row == 0, spread(jnp.where(firsts, 0.0, wake_low), 0), 0.0),
    )
    hx = own[2] - jnp.where(is_top, spread(late_x, 0), 0.0)
    hy = own[1]
    rate_x, rate_y, rate_z, re_x, re_y, re_z = [pack[1 + c] for c in range(6)]
    opened = pack[7]
    ex = pack[0]
    ey = turn(ex, 1)
    ez = wakes
    end = 2 * nx - 1
    ey_i = jnp.where(lane == end, turn(after_x(0, ny), end), turn(ey, -2))
    hz = own[3] - rate_z * ((ey_i - ey) - (upper(ex, spread(ex_q, 0)) - ex))
    hy_i = jnp.where(lane == 1, turn(below[0], 1), turn(hy, 2))
    hz_i = jnp.where(lane == 1, turn(below[1] + jnp.where(is_top, corner, 0.0), 1), turn(hz, 2))
    hx_j, hz_j = lower(hx, spread(hx_n, 0)), lower(hz, spread(hz_n, 0))
    ex_new = opened * ex + re_x * ((hz - hz_j) - hy)
    ey_new = opened * ey + re_y * (hx - (hz - hz_i))
    ez_new = opened * ez + re_z * ((hy - hy_i) - (hx - hx_j))
    ex_row = before_x(3 * ny + 1, 3 * ny + 2)
    ex_m = jnp.sum(jnp.where(lane == row, ex_row, 0.0), axis=1, keepdims=True)
    terms = (
        (-rate_y, ex),
        (jnp.where(lane == 0, turn(below[2], 1), turn(rate_y, 2)), jnp.where(lane == 1, ex_m, turn(ex, 2))),
        (-rate_x, ey),
        (lower(rate_x, spread(rate_xn, 0)), lower(ey, before_y(3 * nx, 3 * nx + 1))),
    )
    ahead_weight, last_weight = tabs[6][:, nz - 2 : nz - 1], tabs[6][:, nz - 1 : nz]
    coefficients = joined([re_z * c for c, _ in terms], group)
    fields = joined([f for _, f in terms] + [ez_new], group)
    mine[0] = turn(coefficients, 1)
    mine[1] = joined((turn(-rate_y, 1), hy, turn(rate_x, 1)), group)
    mine[2] = turn(hy, 1)
    mine[3] = turn(hx, 1)
    two = jnp.where(lane < 4 * group, ahead_weight * coefficients, last_weight)
    two = jnp.where(even, two, fields)
    two = jnp.where(lane < 5 * group, two, 0.0)
    one = joined(
        (
            jnp.where(even, turn(hz, -1), hx),
            hy,
            re_x,
            re_y,
            jnp.where(even, turn(ey_new, -1), ex_new),
        ),
        group,
    )
    sums = jnp.zeros((HEAD, nz), jnp.float32)
    narrow = lanes(sums.shape)
    for g in range(ny // HEAD):
        at = g * group
        moved = turn(wakes[g * HEAD : (g + 1) * HEAD], at)
        sums = jnp.where((narrow >= at) & (narrow < at + group), moved, sums)
    near[0:HEAD] = sums
    near[HEAD : HEAD + ny] = two
    near[HEAD + ny :] = one
    far[0:HEAD] = sums
    far[HEAD:] = two


def outputs(entries, e, h, rate, index, tabs, hx_all, hy_all, below, fixed, xa, xb, ya, yb, e_new, h_new, edges):
    nx, ny, nz = e.shape[1], e.shape[2], e.shape[3]
    plane = (ny, nz)
    _, after_x, _ = from_both(xa, xb, "gx")
    _, after_y, _ = from_both(ya, yb, "gy")
    ex_q = after_y(0, nx)
    is_top = rows(plane) == ny - 1
    hy_m = below[0]
    hz_m = below[1] + jnp.where(is_top, fixed[3, 0:1], 0.0)
    ey_last = after_x(0, ny)
    edges[0] = fixed[0]
    edges[1] = fixed[1]
    edges[2] = fixed[2]
    edges[3] = ex_q

    def step(i, carry):
        hy_m, hz_m = carry
        key = index[i]
        ex, ey = e[0, i], e[1, i]
        ey_i = jnp.where(i == nx - 1, ey_last, e[1, jnp.minimum(i + 1, nx - 1)])
        hx_n, hz_n, hx_top, ex_n = [edges[n, pl.ds(i, 1)] for n in range(4)]
        hx = jnp.where(is_top, hx_top, hx_all[i])
        hy = hy_all[i]
        hz = h[2, i] - look(tabs[2], key) * ((ey_i - ey) - (upper(ex, ex_n) - ex))
        hz_j = lower(hz, hz_n)
        hx_j = lower(hx, hx_n)
        ex_new = ex + look(tabs[3], key) * ((hz - hz_j) - (hy - behind(hy)))
        ey_new = ey + look(tabs[4], key) * ((hx - behind(hx)) - (hz - hz_m))
        ez_new = e[2, i] + rate[2, i] * ((hy - hy_m) - (hx - hx_j))
        for c, value in enumerate((ex_new, ey_new, ez_new)):
            e_new[c, i] = ahead(jnp.where(key < entries, value, 0.0))
        for c, value in enumerate((hx, hy, hz)):
            h_new[c, i] = ahead(value)
        return hy, hz

    lax.fori_loop(0, nx, step, (hy_m, hz_m), unroll=3)


def finish(blocks, e_new, h_new, mine, pack, *refs):
    nx, ny, nz = e_new.shape[1:]
    group = 2 * nx
    tells, (e_out, h_out, wake_out, e_buf, h_buf, wake, every, flat, sems) = refs[:-9], refs[-9:]
    z, size = lax.axis_index("gz"), lax.axis_size("gz")
    inside = z < size - 1
    main, body = slice(HEAD, HEAD + ny), slice(HEAD + ny, HEAD + 2 * ny)
    if blocks is None:
        beyond = lambda at: jnp.where(inside, tells[1][at], 0.0)
    else:
        beyond = lambda at: jnp.where(inside, jnp.where(z % 2 == 0, tells[1][at], tells[blocks - 1][at]), 0.0)
    two, one = beyond(main), beyond(body)
    even = lanes((ny, nz)) % 2 == 0
    product = mine[0] * two
    product = product + turn(product, -2 * group)
    late_ez = turn(product, -1) + turn(product, -group - 1)
    late = mine[1] * two
    late_hy, late_hx = turn(late, -1), turn(late, -2 * group - 1)
    now_ex = turn(one, -4 * group) + turn(one, -2 * group) * (mine[2] + late)
    now_ey = turn(one, 1 - 4 * group) - turn(one, -3 * group) * (mine[3] + turn(late, -2 * group))
    fixes = (
        (-pack[4] * late_hy, now_ex),
        (pack[5] * late_hx, now_ey),
        (late_ez, turn(two, -4 * group)),
        (late_hx, one),
        (late_hy, turn(one, -group)),
        (0.0, turn(one, 1)),
    )
    tail = lanes((ny, nz)) >= nz - 2

    def summed():
        if blocks is None:
            return tells[0][0:HEAD], tells[0][main] * turn(two, -1)
        for m, ref in enumerate(tells):
            every[z ^ m] = ref[0 : HEAD + ny]
        sums = every[0, 0:HEAD]
        total = None
        for b in range(1, blocks):
            sums = sums + every[b, 0:HEAD]
            part = every[b - 1, main] * turn(every[b, main], -1)
            total = part if total is None else total + part
        return sums, total

    copies = []
    for batch in ((5,), (3,), (4,), (6, 2), (1,), (0,)):
        started = []
        for n in batch:
            if n == 6:
                sums, total = summed()
                pairs = total + turn(total, -2 * group)
                sums = jnp.concatenate([turn(sums, -g * group) for g in range(ny // HEAD)], axis=0)
                total = (pairs + turn(pairs, -group)) + (turn(total, -4 * group) + sums)
                flat[...] = total.T
                for i in range(nx):
                    wake[i : i + 1, :] = flat[2 * i : 2 * i + 1, :]
                started.append(pltpu.make_async_copy(wake, wake_out, sems.at[6]))
                continue
            source, buf, out = (e_new, e_buf, e_out) if n < 3 else (h_new, h_buf, h_out)
            c = n % 3
            fix = jnp.where(even, *fixes[n])

            def patch(i, carry):
                moved = turn(fix, nz - 2 - 2 * i)
                buf[c, i] = source[c, i] + jnp.where(tail, moved, 0.0)
                return carry

            if 12 < nx:
                lax.fori_loop(0, nx, patch, 0, unroll=12)
            else:
                for i in range(nx):
                    patch(i, 0)
            started.append(pltpu.make_async_copy(buf.at[c], out.at[c], sems.at[n]))
        for copy in started:
            copy.start()
        copies += started
    for copy in copies:
        copy.wait()


def shards(e_field, h_field, material, coef_index, table_h, table_e, pickup):
    _, nx, ny, nz = e_field.shape
    size_x, size_y, size_z = (lax.axis_size(a) for a in ("gx", "gy", "gz"))
    entries = table_h.shape[0]
    block, whole = f32(nx, ny, nz), f32(3, nx, ny, nz)
    twice = size_x > 2
    body = face_x if twice else lambda *r: face_x(*r[:7], None, *r[7:])
    buffers = [
        pltpu.VMEM((5, ny, nz), jnp.float32),
        pltpu.VMEM((2, ny, nz), jnp.float32),
        pltpu.VMEM((ny, nz), jnp.int32),
        pltpu.VMEM((2, 3, entries), jnp.float32),
        pltpu.VMEM((1, nz), jnp.float32),
        pltpu.SemaphoreType.DMA((7,)),
    ]
    inputs = (e_field, h_field, coef_index, table_h.T, table_e.T, pickup.reshape(1, nz))
    got = call(body, [f32(3 * ny + 8, nz)] * (1 + twice) + [f32(7, ny, nz)], [HBM] * 6, scratch=buffers)(
        *(stay(x) for x in inputs)
    )
    tabs = got[-1]
    xa = paired(got[0], "gx", 0, "gy")
    xb = paired(got[1], "gx", 1, "gy") if twice else xa
    index, rate, pack = call(
        functools.partial(rates, entries),
        [jax.ShapeDtypeStruct((nx, ny, nz), jnp.int32), whole, f32(8, ny, nz)],
        [VMEM] * 4,
    )(e_field, material, coef_index, tabs)
    twice = size_y > 2
    body = face_y if twice else lambda *r: face_y(*r, None)
    got = call(body, [f32(-(-(3 * nx + 1) // 8) * 8, nz)] * (1 + twice), [VMEM] * 7)(
        e_field, h_field, tabs, index, rate, xa, xb
    )
    ya = paired(got[0], "gy", 0, "gx")
    yb = paired(got[1], "gy", 1, "gx") if twice else ya
    hx, hy, below, own = call(
        functools.partial(interior, entries), [block, block, f32(4, ny, nz), f32(4, ny, nz)], [VMEM] * 7
    )(e_field, h_field, rate, index, tabs, xa, xb)
    near, far, mine, fixed = call(
        border,
        [f32(HEAD + 2 * ny, nz), f32(HEAD + ny, nz), f32(4, ny, nz), f32(4, nx, nz)],
        [VMEM] * 11,
    )(e_field, rate, hx, below, pack, own, tabs, xa, xb, ya, yb)
    edges = [pltpu.VMEM((4, nx, nz), jnp.float32)]
    e_new, h_new = call(functools.partial(outputs, entries), [whole, whole], [VMEM] * 13, scratch=edges)(
        e_field, h_field, rate, index, tabs, hx, hy, below, fixed, xa, xb, ya, yb
    )
    blocks = size_z if size_z in (2, 4) else None
    if blocks:
        tells = [near] + [swapped(near if m % 2 else far, "gz", m) for m in range(1, blocks)]
    else:
        route = [(i, i - 1) for i in range(1, size_z)]
        tells = [near, lax.ppermute(near, "gz", route)]
    scratch = [
        pltpu.VMEM((3, nx, ny, nz), jnp.float32),
        pltpu.VMEM((3, nx, ny, nz), jnp.float32),
        pltpu.VMEM((nx, ny), jnp.float32),
        pltpu.VMEM((blocks or 1, HEAD + ny, nz), jnp.float32),
        pltpu.VMEM((nz, ny), jnp.float32),
        pltpu.SemaphoreType.DMA((7,)),
    ]
    e_out, h_out, wake = call(
        functools.partial(finish, blocks),
        [whole, whole, f32(nx, ny)],
        [VMEM] * (4 + len(tells)),
        out_specs=[ANY, ANY, ANY],
        scratch=scratch,
    )(e_new, h_new, mine, pack, *tells)
    if not blocks:
        wake = lax.psum(wake, "gz")
    return e_out, h_out, wake


def solution(mesh):
    return jax.shard_map(
        shards,
        mesh=mesh,
        in_specs=(
            P(None, "gx", "gy", "gz"),
            P(None, "gx", "gy", "gz"),
            P("gx", "gy", "gz"),
            P("gx", "gy", "gz"),
            P(),
            P(),
            P("gz"),
        ),
        out_specs=(P(None, "gx", "gy", "gz"), P(None, "gx", "gy", "gz"), P("gx", "gy")),
        check_vma=False,
    )
```

```python
import functools

import jax
import jax.numpy as jnp
from jax import lax
from jax.experimental import pallas as pl
from jax.experimental.pallas import tpu as pltpu
from jax.sharding import PartitionSpec as P

AXES = ("gz", "gx", "gy")
VMEM = pl.BlockSpec(memory_space=pltpu.VMEM)
SMEM = pl.BlockSpec(memory_space=pltpu.SMEM)
ANY = pl.BlockSpec(memory_space=pl.ANY)
HBM = pl.BlockSpec(memory_space=pltpu.HBM)
LIMIT = 16 * 1024 * 1024


def call(body, outs, in_specs, out_specs=None, scratch=(), cost=1000000):
    return pl.pallas_call(
        body,
        out_shape=outs,
        in_specs=in_specs,
        out_specs=out_specs if out_specs is not None else [VMEM] * len(outs),
        scratch_shapes=scratch,
        compiler_params=pltpu.CompilerParams(vmem_limit_bytes=LIMIT),
        cost_estimate=pl.CostEstimate(flops=cost, bytes_accessed=cost, transcendentals=0),
    )


def stay(x):
    return pltpu.with_memory_space_constraint(x, pltpu.HBM)


def f32(*shape):
    return jax.ShapeDtypeStruct(shape, jnp.float32)


def paired(block, axis, first, spare):
    sizes = [lax.axis_size(a) for a in AXES]
    at, other = AXES.index(axis), AXES.index(spare)
    size = sizes[at]
    pairs = []
    for flat in range(sizes[0] * sizes[1] * sizes[2]):
        where = [flat // (sizes[1] * sizes[2]), flat // sizes[2] % sizes[1], flat % sizes[2]]
        up = where[at] % 2 == first
        target = where[at] + (1 if up else -1)
        if 0 <= target < size:
            where[at] = target
        elif sizes[other] % 2 == 0:
            where[other] = where[other] ^ 1
        else:
            continue
        pairs.append((flat, (where[0] * sizes[1] + where[1]) * sizes[2] + where[2]))
    return lax.ppermute(block, AXES, pairs)


def swapped(block, axis, mask):
    return lax.ppermute(block, axis, [(i, i ^ mask) for i in range(lax.axis_size(axis))])


def from_both(first, second, axis):
    index, size = lax.axis_index(axis), lax.axis_size(axis)
    odd = index % 2 == 1
    is_previous, is_next = index > 0, index < size - 1

    def previous(start, stop):
        got = jnp.where(odd, first[start:stop], second[start:stop])
        return jnp.where(is_previous, got, 0.0)

    def following(start, stop):
        got = jnp.where(odd, second[start:stop], first[start:stop])
        return jnp.where(is_next, got, 0.0)

    return previous, following, is_previous


def lanes(shape):
    return lax.broadcasted_iota(jnp.int32, shape, len(shape) - 1)


def rows(shape):
    return lax.broadcasted_iota(jnp.int32, shape, len(shape) - 2)


def turn(x, amount):
    if isinstance(amount, int):
        amount = amount % x.shape[-1]
    return pltpu.roll(x, amount, axis=x.ndim - 1)


def ahead(x):
    return jnp.where(lanes(x.shape) == x.shape[-1] - 1, 0.0, turn(x, -1))


def behind(x):
    return jnp.where(lanes(x.shape) == 0, 0.0, turn(x, 1))


def upper(x, edge):
    moved = pltpu.roll(x, x.shape[0] - 1, axis=0)
    return jnp.where(rows(x.shape) == x.shape[0] - 1, edge, moved)


def lower(x, edge):
    moved = pltpu.roll(x, 1, axis=0)
    return jnp.where(rows(x.shape) == 0, edge, moved)


def look(table, index):
    return jnp.take_along_axis(table, index, axis=1, mode="promise_in_bounds")


def send(odd, out_a, out_b, start, up, down):
    stop = start + up.shape[0]
    out_a[start:stop] = jnp.where(odd, down, up)
    if out_b is not None:
        out_b[start:stop] = jnp.where(odd, up, down)


def face_x(e, h, coef, th, te, pickup, out_a, out_b, tabs, eb, hb, cb, tb, pb, sems):
    ny, nz = e.shape[2], e.shape[3]
    top = e.shape[1] - 1
    moves = [
        (e.at[:, top], eb.at[0:3]),
        (coef.at[top], cb),
        (th, tb.at[0]),
        (h.at[1:3, top], hb),
        (e.at[1:3, 0], eb.at[3:5]),
        (te, tb.at[1]),
        (pickup, pb),
    ]
    copies = [pltpu.make_async_copy(a, b, sems.at[n]) for n, (a, b) in enumerate(moves)]
    for copy in copies:
        copy.start()
    for copy in copies:
        copy.wait()
    entries = th.shape[1]
    for base in range(2):
        for c in range(3):
            row = jnp.broadcast_to(tb[base, c : c + 1, :], (ny, entries))
            row = jnp.concatenate([row, jnp.zeros((ny, nz - entries), jnp.float32)], axis=1)
            tabs[3 * base + c] = row + turn(row, entries) if base == 0 else row
    tabs[6] = jnp.broadcast_to(pb[...], (ny, nz))
    odd = lax.axis_index("gx") % 2 == 1
    index = cb[...]
    ex, ey, ez = eb[0], eb[1], eb[2]
    part_y = hb[0] - look(tabs[1], index) * ((ahead(ex) - ex) + ez)
    part_z = hb[1] + look(tabs[2], index) * (ey + (upper(ex, 0.0) - ex))
    column = jnp.where(lanes(ex.shape) == rows(ex.shape), ex[:, 0:1], 0.0)
    column = jnp.sum(column, axis=0, keepdims=True)
    key = index.astype(jnp.float32)
    send(odd, out_a, out_b, 0, part_y, eb[3])
    send(odd, out_a, out_b, ny, part_z, eb[4])
    send(odd, out_a, out_b, 2 * ny, key, key)
    send(odd, out_a, out_b, 3 * ny, ex[0:1], ex[0:1])
    send(odd, out_a, out_b, 3 * ny + 1, column, column)


def face_y(e, h, tabs, index, rate, xa, xb, out_a, out_b):
    nx, ny = e.shape[1], e.shape[2]
    last = ny - 1
    before_x, after_x, _ = from_both(xa, xb, "gx")
    odd = lax.axis_index("gy") % 2 == 1
    key = index[:, last, :]
    ex, ey, ez = e[0, :, last, :], e[1, :, last, :], e[2, :, last, :]
    part_x = h[0, :, last, :] + rate[0, :, last, :] * (ez + (ahead(ey) - ey))
    next_y = jnp.concatenate([ey[1:], after_x(last, ny)], axis=0)
    part_z = h[2, :, last, :] - look(tabs[2, :nx], key) * ((next_y - ey) + ex)
    key = key.astype(jnp.float32)
    send(odd, out_a, out_b, 0, part_x, e[0, :, 0, :])
    send(odd, out_a, out_b, nx, part_z, e[2, :, 0, :])
    send(odd, out_a, out_b, 2 * nx, key, key)
    corner = before_x(3 * ny, 3 * ny + 1)
    send(odd, out_a, out_b, 3 * nx, spread(ey, 0), corner)


def spread(x, first):
    n, nz = x.shape
    full = -(-n // 8) * 8
    if full > n:
        x = jnp.concatenate([x, jnp.zeros((full - n, nz), x.dtype)], axis=0)
    moved = pltpu.roll(x, (first + 1) % nz, axis=1, stride=2, stride_axis=0)
    off = lanes(x.shape) - first - 2 * rows(x.shape)
    row = rows(x.shape)
    keep = (off >= 0) & (off < 2) & (row < n)
    return jnp.sum(jnp.where(keep, moved, 0.0), axis=0, keepdims=True)


HEAD = 8


def place(acc, x, first):
    lane = lanes(x.shape)
    moved = turn(x, first + 1)
    return jnp.where((lane >= first) & (lane <= first + 1), moved, acc)


def joined(parts, group):
    lane = lanes(parts[0].shape)
    acc = parts[0]
    for n, part in enumerate(parts[1:], 1):
        acc = jnp.where(lane >= n * group, turn(part, n * group), acc)
    return acc


def rates(entries, e, material, coef, tabs, index, rate, pack):
    nx, ny, nz = e.shape[1], e.shape[2], e.shape[3]
    plane = (ny, nz)
    first_lane = lanes(plane) == 0
    keys = jnp.zeros(plane, jnp.int32)
    exy = jnp.zeros(plane, jnp.float32)

    def step(i, carry):
        keys, exy = carry
        key = coef[i] + entries * material[i]
        index[i] = key
        for n, c in enumerate((0, 1, 5)):
            rate[n, i] = look(tabs[c], key)
        keys = place(keys, key, 2 * i)
        exy = place(exy, jnp.where(first_lane, e[0, i], turn(e[1, i], -1)), 2 * i)
        return keys, exy

    keys, exy = lax.fori_loop(0, nx, step, (keys, exy), unroll=3)
    pack[0] = exy
    for c in range(6):
        pack[1 + c] = look(tabs[c], keys)
    pack[7] = jnp.where(keys < entries, 1.0, 0.0)


def interior(entries, e, h, rate, index, tabs, xa, xb, hx_out, hy_out, below, own):
    nx, ny, nz = e.shape[1], e.shape[2], e.shape[3]
    before_x, after_x, is_before = from_both(xa, xb, "gx")
    plane = (ny, nz)
    first_lane = lanes(plane) == 0
    weight = behind(tabs[6])
    key = before_x(2 * ny, 3 * ny).astype(jnp.int32)
    rate_ym = jnp.where(is_before, look(tabs[1], key), 0.0)
    rate_zm = jnp.where(is_before, look(tabs[2], key), 0.0)
    hy_m = before_x(0, ny) + rate_ym * e[2, 0]
    below[0] = hy_m
    below[1] = before_x(ny, 2 * ny) - rate_zm * e[1, 0]
    below[2] = rate_ym
    below[3] = rate_zm
    ez_last = after_x(ny, 2 * ny)
    wakes = hz = hx_pair = hy_pair = jnp.zeros(plane, jnp.float32)

    def step(i, carry):
        hy_m, wakes, hz, hx_pair, hy_pair = carry
        ex, ey, ez = e[0, i], e[1, i], e[2, i]
        ez_i = jnp.where(i == nx - 1, ez_last, e[2, jnp.minimum(i + 1, nx - 1)])
        hx = h[0, i] - rate[0, i] * ((upper(ez, 0.0) - ez) - (ahead(ey) - ey))
        hy = h[1, i] - rate[1, i] * ((ahead(ex) - ex) - (ez_i - ez))
        hx_out[i] = hx
        hy_out[i] = hy
        ez_new = ez + rate[2, i] * ((hy - hy_m) - (hx - lower(hx, 0.0)))
        wake = jnp.sum(jnp.where(index[i] < entries, weight * ez_new, 0.0), axis=1, keepdims=True)
        wakes = place(wakes, jnp.where(first_lane, ez, wake), 2 * i)
        hz = place(hz, h[2, i], 2 * i)
        hx_pair = place(hx_pair, hx, 2 * i)
        hy_pair = place(hy_pair, hy, 2 * i)
        return hy, wakes, hz, hx_pair, hy_pair

    carry = (hy_m, wakes, hz, hx_pair, hy_pair)
    _, wakes, hz, hx_pair, hy_pair = lax.fori_loop(0, nx, step, carry, unroll=4)
    own[2] = hx_pair
    own[3] = hz
    own[0] = wakes
    own[1] = hy_pair


def border(e, rate, field, below, pack, own, tabs, xa, xb, ya, yb, near, far, raw, fixed):
    nx, ny, nz = e.shape[1], e.shape[2], e.shape[3]
    group = 2 * nx
    last = ny - 1
    before_x, after_x, _ = from_both(xa, xb, "gx")
    before_y, after_y, is_before = from_both(ya, yb, "gy")
    plane = (ny, nz)
    lane, row = lanes(plane), rows(plane)
    even, is_top = lane % 2 == 0, row == last
    key = before_y(2 * nx, 3 * nx).astype(jnp.int32)
    rate_xn = jnp.where(is_before, look(tabs[0, :nx], key), 0.0)
    rate_zn = jnp.where(is_before, look(tabs[2, :nx], key), 0.0)
    hx_n = before_y(0, nx) - rate_xn * e[2, :, 0, :]
    hz_n = before_y(nx, 2 * nx) + rate_zn * e[0, :, 0, :]
    ex_q = after_y(0, nx)
    late_x = rate[0, :, last, :] * after_y(nx, 2 * nx)
    corner = below[3, last:ny] * after_y(3 * nx, 3 * nx + 1)
    fixed[0] = hx_n
    fixed[1] = hz_n
    fixed[2] = field[:, last, :] - late_x
    fixed[3, 0:1] = corner
    weight = behind(tabs[6, :nx])
    wake_low = jnp.sum(weight * rate[2, :, 0, :] * hx_n, axis=1, keepdims=True)
    wake_top = jnp.sum(weight * rate[2, :, last, :] * late_x, axis=1, keepdims=True)
    firsts = lanes(hx_n.shape) == 0
    wakes = own[0] + jnp.where(
        is_top,
        spread(jnp.where(firsts, 0.0, wake_top), 0),
        jnp.where(row == 0, spread(jnp.where(firsts, 0.0, wake_low), 0), 0.0),
    )
    hx = own[2] - jnp.where(is_top, spread(late_x, 0), 0.0)
    hy = own[1]
    rate_x, rate_y, rate_z, re_x, re_y, re_z = [pack[1 + c] for c in range(6)]
    opened = pack[7]
    ex = pack[0]
    ey = turn(ex, 1)
    ez = wakes
    end = 2 * nx - 1
    ey_i = jnp.where(lane == end, turn(after_x(0, ny), end), turn(ey, -2))
    hz = own[3] - rate_z * ((ey_i - ey) - (upper(ex, spread(ex_q, 0)) - ex))
    hy_i = jnp.where(lane == 1, turn(below[0], 1), turn(hy, 2))
    hz_i = jnp.where(lane == 1, turn(below[1] + jnp.where(is_top, corner, 0.0), 1), turn(hz, 2))
    hx_j, hz_j = lower(hx, spread(hx_n, 0)), lower(hz, spread(hz_n, 0))
    ex_new = opened * ex + re_x * ((hz - hz_j) - hy)
    ey_new = opened * ey + re_y * (hx - (hz - hz_i))
    ez_new = opened * ez + re_z * ((hy - hy_i) - (hx - hx_j))
    ex_row = before_x(3 * ny + 1, 3 * ny + 2)
    ex_m = jnp.sum(jnp.where(lane == row, ex_row, 0.0), axis=1, keepdims=True)
    terms = (
        (-rate_y, ex),
        (jnp.where(lane == 0, turn(below[2], 1), turn(rate_y, 2)), jnp.where(lane == 1, ex_m, turn(ex, 2))),
        (-rate_x, ey),
        (lower(rate_x, spread(rate_xn, 0)), lower(ey, before_y(3 * nx, 3 * nx + 1))),
    )
    ahead_weight, last_weight = tabs[6][:, nz - 2 : nz - 1], tabs[6][:, nz - 1 : nz]
    coefficients = joined([re_z * c for c, _ in terms], group)
    fields = joined([f for _, f in terms] + [ez_new], group)
    raw[0] = coefficients
    raw[1] = hx
    two = jnp.where(lane < 4 * group, ahead_weight * coefficients, last_weight)
    two = jnp.where(even, two, fields)
    two = jnp.where(lane < 5 * group, two, 0.0)
    one = joined(
        (
            jnp.where(even, turn(hz, -1), hx),
            hy,
            re_x,
            re_y,
            jnp.where(even, turn(ey_new, -1), ex_new),
        ),
        group,
    )
    sums = jnp.zeros((HEAD, nz), jnp.float32)
    narrow = lanes(sums.shape)
    for g in range(ny // HEAD):
        at = g * group
        moved = turn(wakes[g * HEAD : (g + 1) * HEAD], at)
        sums = jnp.where((narrow >= at) & (narrow < at + group), moved, sums)
    near[0:HEAD] = sums
    near[HEAD : HEAD + ny] = two
    near[HEAD + ny :] = one
    far[0:HEAD] = sums
    far[HEAD:] = two


def outputs(entries, e, h, rate, index, tabs, hx_all, hy_all, below, fixed, xa, xb, ya, yb, raw, pack, own, e_new, h_new, mine, edges):
    nx, ny, nz = e.shape[1], e.shape[2], e.shape[3]
    plane = (ny, nz)
    _, after_x, _ = from_both(xa, xb, "gx")
    _, after_y, _ = from_both(ya, yb, "gy")
    ex_q = after_y(0, nx)
    is_top = rows(plane) == ny - 1
    hy_m = below[0]
    hz_m = below[1] + jnp.where(is_top, fixed[3, 0:1], 0.0)
    ey_last = after_x(0, ny)
    mine[0] = turn(raw[0], 1)
    mine[1] = joined((turn(-pack[2], 1), own[1], turn(pack[1], 1)), 2 * nx)
    mine[2] = turn(own[1], 1)
    mine[3] = turn(raw[1], 1)
    edges[0] = fixed[0]
    edges[1] = fixed[1]
    edges[2] = fixed[2]
    edges[3] = ex_q

    def step(i, carry):
        hy_m, hz_m = carry
        key = index[i]
        ex, ey = e[0, i], e[1, i]
        ey_i = jnp.where(i == nx - 1, ey_last, e[1, jnp.minimum(i + 1, nx - 1)])
        hx_n, hz_n, hx_top, ex_n = [edges[n, pl.ds(i, 1)] for n in range(4)]
        hx = jnp.where(is_top, hx_top, hx_all[i])
        hy = hy_all[i]
        hz = h[2, i] - look(tabs[2], key) * ((ey_i - ey) - (upper(ex, ex_n) - ex))
        hz_j = lower(hz, hz_n)
        hx_j = lower(hx, hx_n)
        ex_new = ex + look(tabs[3], key) * ((hz - hz_j) - (hy - behind(hy)))
        ey_new = ey + look(tabs[4], key) * ((hx - behind(hx)) - (hz - hz_m))
        ez_new = e[2, i] + rate[2, i] * ((hy - hy_m) - (hx - hx_j))
        for c, value in enumerate((ex_new, ey_new, ez_new)):
            e_new[c, i] = ahead(jnp.where(key < entries, value, 0.0))
        for c, value in enumerate((hx, hy, hz)):
            h_new[c, i] = ahead(value)
        return hy, hz

    lax.fori_loop(0, nx, step, (hy_m, hz_m), unroll=3)


def finish(blocks, e_new, h_new, mine, pack, *refs):
    nx, ny, nz = e_new.shape[1:]
    group = 2 * nx
    tells, (e_out, h_out, wake_out, e_buf, h_buf, wake, every, flat, sems) = refs[:-9], refs[-9:]
    z, size = lax.axis_index("gz"), lax.axis_size("gz")
    inside = z < size - 1
    main, body = slice(HEAD, HEAD + ny), slice(HEAD + ny, HEAD + 2 * ny)
    if blocks is None:
        beyond = lambda at: jnp.where(inside, tells[1][at], 0.0)
    else:
        beyond = lambda at: jnp.where(inside, jnp.where(z % 2 == 0, tells[1][at], tells[blocks - 1][at]), 0.0)
    two, one = beyond(main), beyond(body)
    even = lanes((ny, nz)) % 2 == 0
    product = mine[0] * two
    product = product + turn(product, -2 * group)
    late_ez = turn(product, -1) + turn(product, -group - 1)
    late = mine[1] * two
    late_hy, late_hx = turn(late, -1), turn(late, -2 * group - 1)
    now_ex = turn(one, -4 * group) + turn(one, -2 * group) * (mine[2] + late)
    now_ey = turn(one, 1 - 4 * group) - turn(one, -3 * group) * (mine[3] + turn(late, -2 * group))
    fixes = (
        (-pack[4] * late_hy, now_ex),
        (pack[5] * late_hx, now_ey),
        (late_ez, turn(two, -4 * group)),
        (late_hx, one),
        (late_hy, turn(one, -group)),
        (0.0, turn(one, 1)),
    )
    tail = lanes((ny, nz)) >= nz - 2

    def summed():
        if blocks is None:
            return tells[0][0:HEAD], tells[0][main] * turn(two, -1)
        for m, ref in enumerate(tells):
            every[z ^ m] = ref[0 : HEAD + ny]
        sums = every[0, 0:HEAD]
        total = None
        for b in range(1, blocks):
            sums = sums + every[b, 0:HEAD]
            part = every[b - 1, main] * turn(every[b, main], -1)
            total = part if total is None else total + part
        return sums, total

    copies = []
    for batch in ((5,), (6, 3), (4,), (2,), (1,), (0,)):
        started = []
        for n in batch:
            if n == 6:
                sums, total = summed()
                pairs = total + turn(total, -2 * group)
                sums = jnp.concatenate([turn(sums, -g * group) for g in range(ny // HEAD)], axis=0)
                total = (pairs + turn(pairs, -group)) + (turn(total, -4 * group) + sums)
                flat[...] = total.T
                for i in range(nx):
                    wake[i : i + 1, :] = flat[2 * i : 2 * i + 1, :]
                started.append(pltpu.make_async_copy(wake, wake_out, sems.at[6]))
                continue
            source, buf, out = (e_new, e_buf, e_out) if n < 3 else (h_new, h_buf, h_out)
            c = n % 3
            fix = jnp.where(even, *fixes[n])

            def patch(i, carry):
                moved = turn(fix, nz - 2 - 2 * i)
                buf[c, i] = source[c, i] + jnp.where(tail, moved, 0.0)
                return carry

            if 12 < nx:
                lax.fori_loop(0, nx, patch, 0, unroll=12)
            else:
                for i in range(nx):
                    patch(i, 0)
            started.append(pltpu.make_async_copy(buf.at[c], out.at[c], sems.at[n]))
        for copy in started:
            copy.start()
        copies += started
    for copy in copies:
        copy.wait()


def shards(e_field, h_field, material, coef_index, table_h, table_e, pickup):
    _, nx, ny, nz = e_field.shape
    size_x, size_y, size_z = (lax.axis_size(a) for a in ("gx", "gy", "gz"))
    entries = table_h.shape[0]
    block, whole, pair = f32(nx, ny, nz), f32(3, nx, ny, nz), f32(2, ny, nz)
    twice = size_x > 2
    body = face_x if twice else lambda *r: face_x(*r[:7], None, *r[7:])
    buffers = [
        pltpu.VMEM((5, ny, nz), jnp.float32),
        pltpu.VMEM((2, ny, nz), jnp.float32),
        pltpu.VMEM((ny, nz), jnp.int32),
        pltpu.VMEM((2, 3, entries), jnp.float32),
        pltpu.VMEM((1, nz), jnp.float32),
        pltpu.SemaphoreType.DMA((7,)),
    ]
    inputs = (e_field, h_field, coef_index, table_h.T, table_e.T, pickup.reshape(1, nz))
    got = call(body, [f32(3 * ny + 8, nz)] * (1 + twice) + [f32(7, ny, nz)], [HBM] * 6, scratch=buffers)(
        *(stay(x) for x in inputs)
    )
    tabs = got[-1]
    xa = paired(got[0], "gx", 0, "gy")
    xb = paired(got[1], "gx", 1, "gy") if twice else xa
    index, rate, pack = call(
        functools.partial(rates, entries),
        [jax.ShapeDtypeStruct((nx, ny, nz), jnp.int32), whole, f32(8, ny, nz)],
        [VMEM] * 4,
    )(e_field, material, coef_index, tabs)
    twice = size_y > 2
    body = face_y if twice else lambda *r: face_y(*r, None)
    got = call(body, [f32(-(-(3 * nx + 1) // 8) * 8, nz)] * (1 + twice), [VMEM] * 7)(
        e_field, h_field, tabs, index, rate, xa, xb
    )
    ya = paired(got[0], "gy", 0, "gx")
    yb = paired(got[1], "gy", 1, "gx") if twice else ya
    hx, hy, below, own = call(
        functools.partial(interior, entries), [block, block, f32(4, ny, nz), f32(4, ny, nz)], [VMEM] * 7
    )(e_field, h_field, rate, index, tabs, xa, xb)
    near, far, raw, fixed = call(
        border,
        [f32(HEAD + 2 * ny, nz), f32(HEAD + ny, nz), pair, f32(4, nx, nz)],
        [VMEM] * 11,
    )(e_field, rate, hx, below, pack, own, tabs, xa, xb, ya, yb)
    edges = [pltpu.VMEM((4, nx, nz), jnp.float32)]
    e_new, h_new, mine = call(functools.partial(outputs, entries), [whole, whole, f32(4, ny, nz)], [VMEM] * 16, scratch=edges)(
        e_field, h_field, rate, index, tabs, hx, hy, below, fixed, xa, xb, ya, yb, raw, pack, own
    )
    blocks = size_z if size_z in (2, 4) else None
    if blocks:
        tells = [near] + [swapped(near if m % 2 else far, "gz", m) for m in range(1, blocks)]
    else:
        route = [(i, i - 1) for i in range(1, size_z)]
        tells = [near, lax.ppermute(near, "gz", route)]
    scratch = [
        pltpu.VMEM((3, nx, ny, nz), jnp.float32),
        pltpu.VMEM((3, nx, ny, nz), jnp.float32),
        pltpu.VMEM((nx, ny), jnp.float32),
        pltpu.VMEM((blocks or 1, HEAD + ny, nz), jnp.float32),
        pltpu.VMEM((nz, ny), jnp.float32),
        pltpu.SemaphoreType.DMA((7,)),
    ]
    e_out, h_out, wake = call(
        functools.partial(finish, blocks),
        [whole, whole, f32(nx, ny)],
        [VMEM] * (4 + len(tells)),
        out_specs=[ANY, ANY, ANY],
        scratch=scratch,
    )(e_new, h_new, mine, pack, *tells)
    if not blocks:
        wake = lax.psum(wake, "gz")
    return e_out, h_out, wake


def solution(mesh):
    return jax.shard_map(
        shards,
        mesh=mesh,
        in_specs=(
            P(None, "gx", "gy", "gz"),
            P(None, "gx", "gy", "gz"),
            P("gx", "gy", "gz"),
            P("gx", "gy", "gz"),
            P(),
            P(),
            P("gz"),
        ),
        out_specs=(P(None, "gx", "gy", "gz"), P(None, "gx", "gy", "gz"), P("gx", "gy")),
        check_vma=False,
    )
```
